512 devices in a mesh: seq: 32 (over x, y, z_hi), head: 16 (over z_lo, core).
Axes of the slice: x: 4, y: 4, z: 16 (z_hi: 2, z_lo: 8; z = z_hi * 8 + z_lo), core: 2. Of those that a mesh axis runs over, the one named last changes fastest.
Arguments:
- query_rows: bfloat16 [16384, 4096], P('seq', 'head'), may hold values from -100 to 100
- key_rows: bfloat16 [16384, 4096], P('seq', 'head'), may hold values from -4 to 4
- value_rows: bfloat16 [16384, 4096], P('seq', 'head'), may hold values from -6 to 6
- out_grad: bfloat16 [16384, 4096], P('seq', 'head'), may hold values from -6 to 6
- members: int32 [16384], P(('seq', 'head')), may hold values from 0 to 16383, as said below
Outputs:
- attn_out: bfloat16 [16384, 4096], P('seq', 'head')
- query_grad: bfloat16 [16384, 4096], P('seq', 'head')
- key_grad: bfloat16 [16384, 4096], P('seq', 'head')
- value_grad: bfloat16 [16384, 4096], P('seq', 'head')
The draws below stay inside these ranges and needn't reach their ends.
Inputs may be any that keep to these rules, and one draw needn't show every extreme that they name: `members`: every position appears once; the 512 positions of each cluster stand in ascending order. Of the 512 positions of one index of seq a cluster takes 0, 16 or 32, and for each index of seq some clusters take 32. The positions may be sent packed, several to a 32-bit word, or in any narrower integer form that holds them exactly.
All inputs are finite; a program needn't handle non-finite values.
Results may differ from the reference program's by a relative error of at most 0.008.
Values may be sent and summed in bfloat16 or wider, within the bound.
A program may use at most 64 MiB of HBM per device.

```python
import math
import jax
import jax.numpy as jnp
from jax import lax

HD = 128
CLUS = 512
WINDOW = 512
TOK_DEV = 512
SEQ = 16384
HEADS = 32


def cluster_layout(base):
    shards = SEQ // TOK_DEV
    clusters = SEQ // CLUS
    per_dev = clusters // shards
    per_pair = CLUS // shards
    perm_keys = jax.random.split(jax.random.fold_in(base, 11), per_dev)

    def one_order(order_key):
        return jax.random.permutation(order_key, shards)
    orders = jax.vmap(one_order)(perm_keys)
    following = jnp.roll(orders, -1, axis=1)
    owners = jnp.arange(shards)
    high_mark = (owners[None, None, :] == orders[:, :, None]).astype(jnp.int32)
    low_mark = (owners[None, None, :] == following[:, :, None]).astype(jnp.int32)
    counts = per_pair * (1 + high_mark - low_mark)
    counts = jnp.transpose(counts, (1, 2, 0)).reshape(shards, clusters)
    bounds = jnp.cumsum(counts, axis=1)
    positions = jnp.arange(TOK_DEV)
    labels = jnp.sum((bounds[:, None, :] <= positions[None, :, None]).astype(jnp.int32), axis=2)
    shuffle_keys = jax.random.split(jax.random.fold_in(base, 12), shards)

    def shuffled(shuffle_key, label_row):
        return jax.random.permutation(shuffle_key, label_row)
    labels = jax.vmap(shuffled)(shuffle_keys, labels)
    return jnp.argsort(labels.reshape(-1), stable=True).astype(jnp.int32)


def drawn_pair(base):
    heads = HEADS
    shape = (SEQ, heads, HD)
    key_final = jnp.clip(jax.random.normal(jax.random.fold_in(base, 21), shape, jnp.float32), -4.0, 4.0)
    query_final = jnp.clip(jax.random.normal(jax.random.fold_in(base, 23), shape, jnp.float32), -4.0, 4.0)
    return (key_final.reshape(SEQ, heads * HD), query_final.reshape(SEQ, heads * HD))


def draw_members(key, part):
    return cluster_layout(key)


def draw_key_rows(key, part):
    return drawn_pair(key)[0].astype(jnp.bfloat16)


def draw_query_rows(key, part):
    return drawn_pair(key)[1].astype(jnp.bfloat16)


def levels(own_key, dims, cuts, least, top_value):
    level, own = 1.0, jax.random.fold_in(own_key, 6)
    for dim, shards_of in cuts:
        draws = jnp.exp(jax.random.uniform(jax.random.fold_in(own, dim), (shards_of,), jnp.float32, least / len(cuts), top_value / len(cuts)))
        level = level * jnp.repeat(draws, dims[dim] // shards_of).reshape([-1 if axis == dim else 1 for axis in range(len(dims))])
    return level


def scatter_about(stream_key, shape, width, reach, pieces=(), kind=jnp.bfloat16):
    values = jax.random.normal(stream_key, shape, jnp.float32) * width
    if len(pieces) > 0:
        values = levels(stream_key, shape, pieces, -0.22, 0.18) * values
    return jnp.clip(values, min=-reach, max=reach).astype(kind)


def setup_inputs(seed: int = 0) -> dict:
    splits = jax.random.split(jax.random.key(seed), 6)
    return {
        "query_rows": draw_query_rows(jax.random.fold_in(splits[5], 71), 0),
        "key_rows": draw_key_rows(jax.random.fold_in(splits[5], 71), 0),
        "value_rows": scatter_about(splits[2], (SEQ, HEADS * HD), 1.0, 6.0, ((0, 32), (1, 16))),
        "out_grad": scatter_about(splits[3], (SEQ, HEADS * HD), 1.0, 6.0, ((0, 32), (1, 16))),
        "members": draw_members(jax.random.fold_in(splits[5], 71), 0),
    }


def weighted_product(form, left, right):
    return jnp.einsum(form, left.astype(jnp.float32), right.astype(jnp.float32), precision=lax.Precision.HIGHEST)

def attend(query_matrix, input_keys, value_matrix, upstream_gradient, allowed):
    logit_scale = 1.0 / math.sqrt(query_matrix.shape[-1])
    attention_scores = weighted_product('vnw,vtw->vnt', query_matrix, input_keys) * logit_scale
    attention_scores = jnp.where(allowed, attention_scores, -jnp.inf)
    row_max = lax.optimization_barrier(jnp.max(attention_scores, axis=-1, keepdims=True))
    exp_scores = jnp.exp(attention_scores - row_max)
    probability = exp_scores / lax.optimization_barrier(jnp.sum(exp_scores, axis=-1, keepdims=True))
    attention_weights = lax.optimization_barrier(probability.astype(jnp.bfloat16))
    attended_output = weighted_product('yxs,ysl->yxl', attention_weights, value_matrix)
    probability_gradient = weighted_product('vnw,vtw->vnt', upstream_gradient, value_matrix)
    row_delta = lax.optimization_barrier(jnp.sum(probability * probability_gradient, axis=-1, keepdims=True))
    score_gradient = lax.optimization_barrier((probability * (probability_gradient - row_delta) * logit_scale).astype(jnp.bfloat16))
    query_gradient = weighted_product('yxs,ysl->yxl', score_gradient, input_keys)
    key_gradient = weighted_product('ipy,ipg->iyg', score_gradient, query_matrix)
    value_gradient = weighted_product('ipy,ipg->iyg', attention_weights, upstream_gradient)
    return (attended_output, query_gradient, key_gradient, value_gradient)

def window_head(query_matrix, input_keys, value_matrix, upstream_gradient):
    seq_len = query_matrix.shape[0]
    window_len = WINDOW
    blocks = seq_len // window_len
    padding = jnp.zeros((window_len, query_matrix.shape[1]), query_matrix.dtype)
    extended_keys = jnp.concatenate([padding, input_keys], axis=0)
    extended_values = jnp.concatenate([padding, value_matrix], axis=0)

    def framed(extended):
        return jnp.concatenate([extended[:seq_len].reshape(blocks, window_len, -1), extended[window_len:].reshape(blocks, window_len, -1)], axis=1)

    def unframe(blockwise):
        lower_half = blockwise[:, :window_len].reshape(seq_len, -1)
        upper_half = blockwise[:, window_len:].reshape(seq_len, -1)
        return jnp.pad(lower_half, ((0, window_len), (0, 0))) + jnp.pad(upper_half, ((window_len, 0), (0, 0)))
    query_pos = jnp.arange(window_len)[None, :, None]
    key_pos = jnp.arange(2 * window_len)[None, None, :]
    block_pos = jnp.arange(blocks)[:, None, None]
    allowed = (key_pos > query_pos) & (key_pos <= query_pos + window_len) & (block_pos * window_len + key_pos >= window_len)
    attended_output, query_gradient, key_gradient, value_gradient = attend(query_matrix.reshape(blocks, window_len, -1), framed(extended_keys), framed(extended_values), upstream_gradient.reshape(blocks, window_len, -1), allowed)
    return (attended_output.reshape(seq_len, -1).astype(jnp.bfloat16), query_gradient.reshape(seq_len, -1).astype(jnp.bfloat16), unframe(key_gradient)[window_len:].astype(jnp.bfloat16), unframe(value_gradient)[window_len:].astype(jnp.bfloat16))

def reference(query_rows, key_rows, value_rows, out_grad, members):
    seq_len = query_rows.shape[0]
    heads_half = query_rows.shape[1] // (2 * HD)

    def split_heads(array):
        return array.reshape(seq_len, heads_half, 2, HD)

    def window_slice(array):
        return jnp.transpose(split_heads(array)[:, :, 0], (1, 0, 2))

    def cluster_slice(array):
        return split_heads(array)[:, :, 1]

    def window_pack(packed):
        return window_head(packed[0], packed[1], packed[2], packed[3])
    window_results = lax.map(window_pack, (window_slice(query_rows), window_slice(key_rows), window_slice(value_rows), window_slice(out_grad)))
    window_stack = jnp.stack([jnp.transpose(result, (1, 0, 2)) for result in window_results])
    route_query = cluster_slice(query_rows)
    route_key = cluster_slice(key_rows)
    route_value = cluster_slice(value_rows)
    route_grad = cluster_slice(out_grad)
    member_table = members.reshape(-1, CLUS)
    causal = (jnp.arange(CLUS)[:, None] >= jnp.arange(CLUS)[None, :])[None]

    def one_cluster(indices):
        group_query = jnp.transpose(route_query[indices], (1, 0, 2))
        group_key = jnp.transpose(route_key[indices], (1, 0, 2))
        group_value = jnp.transpose(route_value[indices], (1, 0, 2))
        group_grad = jnp.transpose(route_grad[indices], (1, 0, 2))
        results = attend(group_query, group_key, group_value, group_grad, causal)
        return jnp.stack(results).astype(jnp.bfloat16)
    gathered = lax.map(one_cluster, member_table)
    ordered = jnp.transpose(gathered, (1, 0, 3, 2, 4)).reshape(4, seq_len, heads_half, HD)
    placed = jnp.zeros_like(ordered).at[:, members].set(ordered)
    combined = jnp.stack([window_stack, placed], axis=3).reshape(4, seq_len, heads_half * 2 * HD)
    return (combined[0], combined[1], combined[2], combined[3])
```

```python
import math

import jax
import jax.numpy as jnp
from jax import lax
from jax.experimental import pallas as pl
from jax.experimental.pallas import tpu as pltpu
from jax.sharding import Mesh
from jax.sharding import PartitionSpec as P

HD = 128
TOK = 512
CAP = 32
NX, NY, NZH, NZL, NCORE = 4, 4, 2, 8, 2
NPLANE = NX * NY * NCORE
NCOL = NZH * NZL
SLOTS = NPLANE * CAP
AXES = ("x", "y", "zh", "zl", "core")
MESH = pl.DeviceIdType.MESH
F32 = jnp.float32
BF16 = jnp.bfloat16
SCALE = 1.0 / math.sqrt(HD)


def iota(shape, dim):
    return lax.broadcasted_iota(jnp.int32, shape, dim)


def iotaf(shape, dim):
    return iota(shape, dim).astype(F32)


def dot_nn(a, b):
    return lax.dot_general(a, b, (((1,), (0,)), ((), ())), preferred_element_type=F32)


def dot_nt(a, b):
    return lax.dot_general(a, b, (((1,), (1,)), ((), ())), preferred_element_type=F32)


def dot_tn(a, b):
    return lax.dot_general(a, b, (((0,), (0,)), ((), ())), preferred_element_type=F32)


def attend_rows(query, grad, parts):
    scores = [jnp.where(mask, dot_nt(key, query) * SCALE, -jnp.inf) for key, _, mask in parts]
    top = None
    for score in scores:
        part_top = jnp.max(score, axis=0, keepdims=True)
        top = part_top if top is None else jnp.maximum(top, part_top)
    terms = [jnp.exp(score - top) for score in scores]
    total = sum(jnp.sum(term, axis=0, keepdims=True) for term in terms)
    inverse = 1.0 / total
    probs = [term * inverse for term in terms]
    weights = [prob.astype(BF16) for prob in probs]
    grad_probs = [dot_nt(value, grad) for _, value, _ in parts]
    delta = sum(
        jnp.sum(prob * grad_prob, axis=0, keepdims=True)
        for prob, grad_prob in zip(probs, grad_probs)
    )
    grad_scores = [
        (prob * (grad_prob - delta) * SCALE).astype(BF16)
        for prob, grad_prob in zip(probs, grad_probs)
    ]
    out = sum(dot_tn(value, weight) for (_, value, _), weight in zip(parts, weights))
    grad_query = sum(dot_tn(key, gs) for (key, _, _), gs in zip(parts, grad_scores))
    return out.T, grad_query.T, weights, grad_scores, (top, inverse, delta)


def kernel(
    q_ref, k_ref, v_ref, g_ref, mem_ref,
    o_ref, dq_ref, dk_ref, dv_ref,
    piece, colbuf, tile, planebuf, lists,
    xbuf, rim, stat_out, stat_in,
    pack, pack_t, sort, sort_t,
    sbuf, rbuf, xc, res, sbuf2, rbuf2, bsend, brecv,
    col_s, col_r, plane_s, plane_r, swap_s, swap_r, rim_s, rim_r, stat_s, stat_r,
    fwd_s, fwd_r, bwd_s, bwd_r, back_s, back_r,
):
    x, y, zh, zl, core = [lax.axis_index(a) for a in AXES]
    z = zh * NZL + zl
    i = x * NY + y
    p = core * (NX * NY) + i
    seq = i * 2 + zh

    def in_plane(index):
        spot = lax.rem(index, NX * NY)
        return (spot // NY, lax.rem(spot, NY), zh, zl, index // (NX * NY))

    def in_column(depth):
        return (x, y, depth // NZL, lax.rem(depth, NZL), core)

    def of_seq(index):
        spot = index // 2
        return (spot // NY, lax.rem(spot, NY), lax.rem(index, 2), zl, core)

    swap_dev = (x, y, 1 - zh, zl, 1 - core)
    next_dev = of_seq(lax.rem(seq + 1, 32))
    prev_dev = of_seq(lax.rem(seq + 31, 32))
    far_dev = of_seq(lax.rem(seq + 31 + 2 * zh, 32))
    swapped = zh != core

    def remote(src, dst, send, recv, device):
        return pltpu.make_async_remote_copy(
            src_ref=src, dst_ref=dst, send_sem=send, recv_sem=recv,
            device_id=device, device_id_type=MESH,
        )

    def wait_bytes(ref, sem):
        pltpu.make_async_copy(ref, ref, sem).wait()

    h = zl * 2 + core
    lane_part = iota((1, 128), 1) // 32
    stat_out[...] = jnp.zeros_like(stat_out)
    piece[0] = jnp.where(lane_part == lax.rem(h, 4), mem_ref[...], 0)

    barrier = pltpu.get_barrier_semaphore()

    def greet(device):
        pl.semaphore_signal(barrier, inc=1, device_id=device, device_id_type=MESH)

    @pl.loop(1, NCOL)
    def _(d):
        greet(in_column(lax.rem(z + d, NCOL)))

    @pl.loop(1, NPLANE)
    def _(d):
        greet(in_plane(lax.rem(p + d, NPLANE)))

    greet(far_dev)
    greet(swap_dev)
    pl.semaphore_wait(barrier, NCOL - 1 + NPLANE - 1 + 2)

    @pl.loop(1, NCOL)
    def _(d):
        remote(
            piece.at[0], colbuf.at[z], col_s, col_r, in_column(lax.rem(z + d, NCOL))
        ).start()

    inputs = (q_ref, k_ref, v_ref, g_ref)
    route = pl.ds(HD, HD)
    local = pl.ds(0, HD)
    swaps = [
        remote(
            inputs[t].at[:, route],
            xbuf.at[t // 2, :, pl.ds((t % 2) * HD, HD)],
            swap_s.at[t], swap_r.at[t], swap_dev,
        )
        for t in range(4)
    ]
    rims = [
        remote(ref.at[:, local], rim.at[t], rim_s.at[t], rim_r.at[t], device)
        for t, (ref, device) in enumerate(
            ((k_ref, next_dev), (v_ref, next_dev), (q_ref, prev_dev), (g_ref, prev_dev))
        )
    ]

    @pl.when(swapped)
    def _():
        for copy in swaps:
            copy.start()
        for copy in rims:
            copy.start()

    @pl.when(jnp.logical_not(swapped))
    def _():
        for t in range(4):
            xbuf[t // 2, :, (t % 2) * HD : (t % 2 + 1) * HD] = inputs[t][:, HD:]

    colbuf[pl.ds(z, 1)] = piece[...]
    wait_bytes(colbuf.at[pl.ds(0, NCOL - 1)], col_r)
    for row in range(8):
        first = (row // 4) * NZL + (row % 4) * 2
        tile[row : row + 1, :] = colbuf[first] + colbuf[first + 1]

    @pl.loop(1, NPLANE)
    def _(d):
        remote(
            tile, planebuf.at[p], plane_s, plane_r, in_plane(lax.rem(p + d, NPLANE))
        ).start()

    planebuf[pl.ds(p, 1)] = tile[...][None]
    wait_bytes(planebuf.at[pl.ds(0, NPLANE - 1)], plane_r)
    for row in range(8):
        rows = planebuf[0:16, row, :] + planebuf[16:32, row, :]
        half, group = row // 4, row % 4
        lists[half * 16 : half * 16 + 16, group * 128 : (group + 1) * 128] = rows.astype(F32)

    base = ((2 * i + core) * TOK).astype(F32)

    @pl.loop(0, 8)
    def _(group):
        token_row = jnp.zeros((1, 128), F32)
        for member in range(4):
            cluster = group * 4 + member
            row = lists[pl.ds(cluster, 1), :]
            start = jnp.sum(jnp.where(row < base, 1.0, 0.0), axis=1, keepdims=True)
            wanted = iotaf((CAP, TOK), 0) + start
            picked = jnp.where(iotaf((CAP, TOK), 1) == wanted, row + 1.0, 0.0)
            token = jnp.sum(picked, axis=1, keepdims=True) - (1.0 + base)
            onehot = jnp.where(iotaf((CAP, TOK), 1) == token, 1.0, 0.0)
            pack[pl.ds(pl.multiple_of(cluster * CAP, CAP), CAP), :] = onehot.astype(BF16)
            placed = iota((CAP, 128), 1) == iota((CAP, 128), 0) + CAP * member
            token_row += jnp.sum(jnp.where(placed, token, 0.0), axis=0, keepdims=True)
        onehot = jnp.where(iotaf((TOK, 128), 0) == token_row, 1.0, 0.0)
        pack_t[:, pl.ds(pl.multiple_of(group * 128, 128), 128)] = onehot.astype(BF16)

    own = lists[pl.ds(p, 1), :].astype(jnp.int32)
    block = own >> 9
    same = iota((NPLANE, TOK), 0) == block
    earlier = jnp.sum(
        jnp.where(block < iota((NPLANE, TOK), 0), 1.0, 0.0), axis=1, keepdims=True
    )
    run_start = jnp.sum(jnp.where(same, earlier, 0.0), axis=0, keepdims=True)
    source = ((block & 1) * 16 + (block >> 1)) * CAP
    slot_row = source.astype(F32) + iotaf((1, TOK), 1) - run_start
    for part in range(8):
        rows = iotaf((128, TOK), 0) + part * 128.0
        sort_t[part * 128 : (part + 1) * 128, :] = jnp.where(rows == slot_row, 1.0, 0.0).astype(BF16)
    for part in range(4):
        piece_row = slot_row[:, part * 128 : (part + 1) * 128]
        diagonal = iota((128, 128), 0) == iota((128, 128), 1)
        slot_col = jnp.sum(jnp.where(diagonal, piece_row, 0.0), axis=1, keepdims=True)
        onehot = jnp.where(iotaf((128, SLOTS), 1) == slot_col, 1.0, 0.0)
        sort[part * 128 : (part + 1) * 128, :] = onehot.astype(BF16)

    @pl.when(jnp.logical_not(swapped))
    def _():
        for copy in rims:
            copy.start()

    def exchange(from_buf, to_buf, g, send, recv):
        @pl.loop(1, NPLANE)
        def _(d):
            other = lax.rem(p + d, NPLANE)
            remote(
                from_buf.at[g, other], to_buf.at[g, p], send.at[g], recv.at[g], in_plane(other)
            ).start()

        to_buf[g, pl.ds(p, 1)] = from_buf[g, pl.ds(p, 1)]

    def fill(to_buf, g, matrix, data):
        for part in range(4):
            rows = dot_nn(matrix[part * 256 : (part + 1) * 256, :], data)
            to_buf[g, part * 8 : (part + 1) * 8] = rows.astype(BF16).reshape(8, CAP, 2 * HD)

    for g in range(2):

        @pl.when(swapped)
        def _():
            swaps[2 * g].wait_recv()
            swaps[2 * g + 1].wait_recv()

        fill(sbuf, g, pack, xbuf[g])
        exchange(sbuf, rbuf, g, fwd_s, fwd_r)

    for g in range(2):
        wait_bytes(rbuf.at[g, pl.ds(0, NPLANE - 1)], fwd_r.at[g])
        xc[g] = dot_nn(sort[...], rbuf[g].reshape(SLOTS, 2 * HD)).astype(BF16)

    half = TOK // 2

    def cluster_rows(qb):
        lo = qb * half
        nk = lo + half
        query = xc[0, lo : lo + half, :HD]
        grad = xc[1, lo : lo + half, HD:]
        key = xc[0, :nk, HD:]
        value = xc[1, :nk, :HD]
        mask = iota((nk, half), 0) <= iota((nk, half), 1) + lo
        out, grad_query, weights, grad_scores, _ = attend_rows(query, grad, [(key, value, mask)])
        res[0, lo : lo + half, :HD] = out.astype(BF16)
        res[0, lo : lo + half, HD:] = grad_query.astype(BF16)
        return dot_nn(grad_scores[0], query), dot_nn(weights[0], grad)

    dk_a, dv_a = cluster_rows(0)
    dk_b, dv_b = cluster_rows(1)
    fill(sbuf2, 0, sort_t, res[0])
    exchange(sbuf2, rbuf2, 0, bwd_s, bwd_r)
    res[1, :half, :HD] = (dk_a + dk_b[:half]).astype(BF16)
    res[1, half:, :HD] = dk_b[half:].astype(BF16)
    res[1, :half, HD:] = (dv_a + dv_b[:half]).astype(BF16)
    res[1, half:, HD:] = dv_b[half:].astype(BF16)
    fill(sbuf2, 1, sort_t, res[1])
    exchange(sbuf2, rbuf2, 1, bwd_s, bwd_r)

    rims[0].wait_recv()
    rims[1].wait_recv()
    hide = jnp.where(seq == 0, 4 * TOK, 0)
    own_parts = []
    for qb in range(2):
        lo = qb * half
        nk = lo + half
        query = q_ref[lo : lo + half, :HD]
        grad = g_ref[lo : lo + half, :HD]
        behind = TOK - lo
        rim_mask = iota((behind, half), 0) + lo > iota((behind, half), 1) + lo + hide
        own_mask = iota((nk, half), 0) <= iota((nk, half), 1) + lo
        out, grad_query, weights, grad_scores, stats = attend_rows(
            query,
            grad,
            [
                (rim[0, lo:, :], rim[1, lo:, :], rim_mask),
                (k_ref[:nk, :HD], v_ref[:nk, :HD], own_mask),
            ],
        )
        o_ref[lo : lo + half, :HD] = out.astype(BF16)
        dq_ref[lo : lo + half, :HD] = grad_query.astype(BF16)
        for row, stat in enumerate(stats):
            stat_out[row : row + 1, lo : lo + half] = stat
        own_parts.append((dot_nn(grad_scores[1], query), dot_nn(weights[1], grad)))
    stats_copy = remote(stat_out, stat_in, stat_s, stat_r, prev_dev)
    stats_copy.start()

    targets = ((o_ref, dq_ref), (dk_ref, dv_ref))
    backs = [
        remote(bsend.at[g], brecv.at[g], back_s.at[g], back_r.at[g], swap_dev) for g in range(2)
    ]
    for g in range(2):
        wait_bytes(rbuf2.at[g, pl.ds(0, NPLANE - 1)], bwd_r.at[g])
        bsend[g] = dot_nn(pack_t[...], rbuf2[g].reshape(SLOTS, 2 * HD)).astype(BF16)

        @pl.when(swapped)
        def _():
            backs[g].start()

        @pl.when(jnp.logical_not(swapped))
        def _():
            targets[g][0][:, HD:] = bsend[g, :, :HD]
            targets[g][1][:, HD:] = bsend[g, :, HD:]

    rims[2].wait_recv()
    rims[3].wait_recv()
    stats_copy.wait_recv()
    last = jnp.where(seq == 31, 4 * TOK, 0)
    next_parts = []
    for qb in range(2):
        lo = qb * half
        behind = TOK - lo
        query = rim[2, lo : lo + half, :]
        grad = rim[3, lo : lo + half, :]
        key = k_ref[lo:, :HD]
        value = v_ref[lo:, :HD]
        mask = iota((behind, half), 0) > iota((behind, half), 1) + last
        score = jnp.where(mask, dot_nt(key, query) * SCALE, -jnp.inf)
        top, inverse, delta = [stat_in[row : row + 1, lo : lo + half] for row in range(3)]
        prob = jnp.exp(score - top) * inverse
        weight = prob.astype(BF16)
        grad_score = (prob * (dot_nt(value, grad) - delta) * SCALE).astype(BF16)
        next_parts.append((dot_nn(grad_score, query), dot_nn(weight, grad)))
    for t, ref in enumerate((dk_ref, dv_ref)):
        own_a, own_b = own_parts[0][t], own_parts[1][t]
        next_a, next_b = next_parts[0][t], next_parts[1][t]
        ref[:half, :HD] = (own_a + own_b[:half] + next_a[:half]).astype(BF16)
        ref[half:, :HD] = (own_b[half:] + next_a[half:] + next_b).astype(BF16)

    @pl.when(swapped)
    def _():
        for g in range(2):
            backs[g].wait_recv()
            targets[g][0][:, HD:] = brecv[g, :, :HD]
            targets[g][1][:, HD:] = brecv[g, :, HD:]
        for copy in swaps:
            copy.wait_send()
        for copy in backs:
            copy.wait_send()

    for copy in rims:
        copy.wait_send()
    stats_copy.wait_send()
    wait_bytes(colbuf.at[pl.ds(0, NCOL - 1)], col_s)
    wait_bytes(planebuf.at[pl.ds(0, NPLANE - 1)], plane_s)
    for g in range(2):
        wait_bytes(rbuf.at[g, pl.ds(0, NPLANE - 1)], fwd_s.at[g])
        wait_bytes(rbuf2.at[g, pl.ds(0, NPLANE - 1)], bwd_s.at[g])


def on_device(query_rows, key_rows, value_rows, out_grad, members):
    vmem = pl.BlockSpec(memory_space=pltpu.VMEM)
    shape = jax.ShapeDtypeStruct((TOK, 2 * HD), BF16)
    padded = pltpu.VMEM((2, NPLANE, CAP, 2 * HD), BF16)
    pair = pltpu.VMEM((2, TOK, 2 * HD), BF16)
    dma = pltpu.SemaphoreType.DMA
    return pl.pallas_call(
        kernel,
        out_shape=(shape,) * 4,
        in_specs=[vmem] * 5,
        out_specs=(vmem,) * 4,
        scratch_shapes=[
            pltpu.VMEM((1, 1, 128), jnp.int32),
            pltpu.VMEM((NCOL, 1, 128), jnp.int32),
            pltpu.VMEM((8, 128), jnp.int32),
            pltpu.VMEM((NPLANE, 8, 128), jnp.int32),
            pltpu.VMEM((NPLANE, TOK), F32),
            pair,
            pltpu.VMEM((4, TOK, HD), BF16),
            pltpu.VMEM((8, TOK), F32),
            pltpu.VMEM((8, TOK), F32),
            pltpu.VMEM((SLOTS, TOK), BF16),
            pltpu.VMEM((TOK, SLOTS), BF16),
            pltpu.VMEM((TOK, SLOTS), BF16),
            pltpu.VMEM((SLOTS, TOK), BF16),
            padded, padded, pair, pair, padded, padded, pair, pair,
            dma, dma, dma, dma, dma((4,)), dma((4,)), dma((4,)), dma((4,)), dma, dma,
            dma((2,)), dma((2,)), dma((2,)), dma((2,)), dma((2,)), dma((2,)),
        ],
        compiler_params=pltpu.CompilerParams(collective_id=0, has_side_effects=True),
    )(query_rows, key_rows, value_rows, out_grad, jnp.tile(members, 4).reshape(1, 128))


def solution(mesh):
    fine = Mesh(mesh.devices.reshape(NX, NY, NZH, NZL, NCORE), AXES)
    rows, cols = ("x", "y", "zh"), ("zl", "core")
    spec = P(rows, cols)
    return jax.shard_map(
        on_device,
        mesh=fine,
        in_specs=(spec, spec, spec, spec, P(AXES)),
        out_specs=(spec,) * 4,
        check_vma=False,
    )
```

```python
import math

import jax
import jax.numpy as jnp
from jax import lax
from jax.experimental import pallas as pl
from jax.experimental.pallas import tpu as pltpu
from jax.sharding import Mesh
from jax.sharding import PartitionSpec as P

HD = 128
TOK = 512
CAP = 32
NX, NY, NZH, NZL, NCORE = 4, 4, 2, 8, 2
NPLANE = NX * NY * NCORE
NCOL = NZH * NZL
SLOTS = NPLANE * CAP
AXES = ("x", "y", "zh", "zl", "core")
MESH = pl.DeviceIdType.MESH
F32 = jnp.float32
BF16 = jnp.bfloat16
SCALE = 1.0 / math.sqrt(HD)


def iota(shape, dim):
    return lax.broadcasted_iota(jnp.int32, shape, dim)


def iotaf(shape, dim):
    return iota(shape, dim).astype(F32)


def dot_nn(a, b):
    return lax.dot_general(a, b, (((1,), (0,)), ((), ())), preferred_element_type=F32)


def dot_nt(a, b):
    return lax.dot_general(a, b, (((1,), (1,)), ((), ())), preferred_element_type=F32)


def dot_tn(a, b):
    return lax.dot_general(a, b, (((0,), (0,)), ((), ())), preferred_element_type=F32)


def attend_rows(query, grad, parts):
    scores = [jnp.where(mask, dot_nt(key, query) * SCALE, -jnp.inf) for key, _, mask in parts]
    top = None
    for score in scores:
        part_top = jnp.max(score, axis=0, keepdims=True)
        top = part_top if top is None else jnp.maximum(top, part_top)
    terms = [jnp.exp(score - top) for score in scores]
    total = sum(jnp.sum(term, axis=0, keepdims=True) for term in terms)
    inverse = 1.0 / total
    probs = [term * inverse for term in terms]
    weights = [prob.astype(BF16) for prob in probs]
    grad_probs = [dot_nt(value, grad) for _, value, _ in parts]
    delta = sum(
        jnp.sum(prob * grad_prob, axis=0, keepdims=True)
        for prob, grad_prob in zip(probs, grad_probs)
    )
    grad_scores = [
        (prob * (grad_prob - delta) * SCALE).astype(BF16)
        for prob, grad_prob in zip(probs, grad_probs)
    ]
    out = sum(dot_tn(value, weight) for (_, value, _), weight in zip(parts, weights))
    grad_query = sum(dot_tn(key, gs) for (key, _, _), gs in zip(parts, grad_scores))
    return out.T, grad_query.T, weights, grad_scores, (top, inverse, delta)


def kernel(
    q_ref, k_ref, v_ref, g_ref, mem_ref,
    o_ref, dq_ref, dk_ref, dv_ref,
    piece, colbuf, tile, planebuf, lists,
    xbuf, rim, stat_out, stat_in,
    pack, pack_t, sort, sort_t,
    sbuf, rbuf, xc, res, sbuf2, rbuf2, bsend, brecv,
    col_s, col_r, plane_s, plane_r, swap_s, swap_r, rim_s, rim_r, stat_s, stat_r,
    fwd_s, fwd_r, bwd_s, bwd_r, back_s, back_r,
):
    x, y, zh, zl, core = [lax.axis_index(a) for a in AXES]
    z = zh * NZL + zl
    i = x * NY + y
    p = core * (NX * NY) + i
    seq = i * 2 + zh

    def in_plane(index):
        spot = lax.rem(index, NX * NY)
        return (spot // NY, lax.rem(spot, NY), zh, zl, index // (NX * NY))

    def in_column(depth):
        return (x, y, depth // NZL, lax.rem(depth, NZL), core)

    def of_seq(index):
        spot = index // 2
        return (spot // NY, lax.rem(spot, NY), lax.rem(index, 2), zl, core)

    swap_dev = (x, y, 1 - zh, zl, 1 - core)
    next_dev = of_seq(lax.rem(seq + 1, 32))
    prev_dev = of_seq(lax.rem(seq + 31, 32))
    far_dev = of_seq(lax.rem(seq + 31 + 2 * zh, 32))
    swapped = zh != core

    def remote(src, dst, send, recv, device):
        return pltpu.make_async_remote_copy(
            src_ref=src, dst_ref=dst, send_sem=send, recv_sem=recv,
            device_id=device, device_id_type=MESH,
        )

    def wait_bytes(ref, sem):
        pltpu.make_async_copy(ref, ref, sem).wait()

    h = zl * 2 + core
    stat_out[...] = jnp.zeros_like(stat_out)
    piece[0] = jnp.zeros((1, 128), jnp.int32)
    for quarter in range(4):

        @pl.when(lax.rem(h, 4) == quarter)
        def _():
            piece[0, :, quarter * 32 : quarter * 32 + 32] = mem_ref[...]


    barrier = pltpu.get_barrier_semaphore()

    def greet(device):
        pl.semaphore_signal(barrier, inc=1, device_id=device, device_id_type=MESH)

    greet(swap_dev)
    greet(far_dev)

    @pl.loop(1, NCOL)
    def _(d):
        greet(in_column(lax.rem(z + d, NCOL)))

    @pl.loop(1, NPLANE)
    def _(d):
        greet(in_plane(lax.rem(p + d, NPLANE)))

    pl.semaphore_wait(barrier, NCOL - 1 + NPLANE - 1 + 2)

    @pl.loop(1, NCOL)
    def _(d):
        remote(
            piece.at[0], colbuf.at[z], col_s, col_r, in_column(lax.rem(z + d, NCOL))
        ).start()

    inputs = (q_ref, k_ref, v_ref, g_ref)
    route = pl.ds(HD, HD)
    local = pl.ds(0, HD)
    swaps = [
        remote(
            inputs[t].at[:, route],
            xbuf.at[t // 2, :, pl.ds((t % 2) * HD, HD)],
            swap_s.at[t], swap_r.at[t], swap_dev,
        )
        for t in range(4)
    ]
    rims = [
        remote(ref.at[:, local], rim.at[t], rim_s.at[t], rim_r.at[t], device)
        for t, (ref, device) in enumerate(
            ((k_ref, next_dev), (v_ref, next_dev), (q_ref, prev_dev), (g_ref, prev_dev))
        )
    ]

    @pl.when(swapped)
    def _():
        for copy in swaps:
            copy.start()

    @pl.when(jnp.logical_not(swapped))
    def _():
        for t in range(4):
            xbuf[t // 2, :, (t % 2) * HD : (t % 2 + 1) * HD] = inputs[t][:, HD:]

    colbuf[pl.ds(z, 1)] = piece[...]
    wait_bytes(colbuf.at[pl.ds(0, NCOL - 1)], col_r)
    for row in range(8):
        first = (row // 4) * NZL + (row % 4) * 2
        tile[row : row + 1, :] = colbuf[first] + colbuf[first + 1]

    @pl.loop(1, NPLANE)
    def _(d):
        remote(
            tile, planebuf.at[p], plane_s, plane_r, in_plane(lax.rem(p + d, NPLANE))
        ).start()

    planebuf[pl.ds(p, 1)] = tile[...][None]
    wait_bytes(planebuf.at[pl.ds(0, NPLANE - 1)], plane_r)
    for row in range(8):
        rows = planebuf[0:16, row, :] + planebuf[16:32, row, :]
        half, group = row // 4, row % 4
        lists[half * 16 : half * 16 + 16, group * 128 : (group + 1) * 128] = rows.astype(F32)

    base = ((2 * i + core) * TOK).astype(F32)

    @pl.loop(0, 8)
    def _(group):
        token_row = jnp.zeros((1, 128), F32)
        for member in range(4):
            cluster = group * 4 + member
            row = lists[pl.ds(cluster, 1), :]
            start = jnp.sum(jnp.where(row < base, 1.0, 0.0), axis=1, keepdims=True)
            wanted = iotaf((CAP, TOK), 0) + start
            picked = jnp.where(iotaf((CAP, TOK), 1) == wanted, row + 1.0, 0.0)
            token = jnp.sum(picked, axis=1, keepdims=True) - (1.0 + base)
            onehot = jnp.where(iotaf((CAP, TOK), 1) == token, 1.0, 0.0)
            pack[pl.ds(pl.multiple_of(cluster * CAP, CAP), CAP), :] = onehot.astype(BF16)
            placed = iota((CAP, 128), 1) == iota((CAP, 128), 0) + CAP * member
            token_row += jnp.sum(jnp.where(placed, token, 0.0), axis=0, keepdims=True)
        onehot = jnp.where(iotaf((TOK, 128), 0) == token_row, 1.0, 0.0)
        pack_t[:, pl.ds(pl.multiple_of(group * 128, 128), 128)] = onehot.astype(BF16)

    own = lists[pl.ds(p, 1), :].astype(jnp.int32)
    block = own >> 9
    same = iota((NPLANE, TOK), 0) == block
    earlier = jnp.sum(
        jnp.where(block < iota((NPLANE, TOK), 0), 1.0, 0.0), axis=1, keepdims=True
    )
    run_start = jnp.sum(jnp.where(same, earlier, 0.0), axis=0, keepdims=True)
    source = ((block & 1) * 16 + (block >> 1)) * CAP
    slot_row = source.astype(F32) + iotaf((1, TOK), 1) - run_start
    for part in range(8):
        rows = iotaf((128, TOK), 0) + part * 128.0
        sort_t[part * 128 : (part + 1) * 128, :] = jnp.where(rows == slot_row, 1.0, 0.0).astype(BF16)
    for part in range(4):
        piece_row = slot_row[:, part * 128 : (part + 1) * 128]
        diagonal = iota((128, 128), 0) == iota((128, 128), 1)
        slot_col = jnp.sum(jnp.where(diagonal, piece_row, 0.0), axis=1, keepdims=True)
        onehot = jnp.where(iotaf((128, SLOTS), 1) == slot_col, 1.0, 0.0)
        sort[part * 128 : (part + 1) * 128, :] = onehot.astype(BF16)


    def exchange(from_buf, to_buf, g, send, recv):
        @pl.loop(1, NPLANE)
        def _(d):
            other = lax.rem(p + d, NPLANE)
            remote(
                from_buf.at[g, other], to_buf.at[g, p], send.at[g], recv.at[g], in_plane(other)
            ).start()

        to_buf[g, pl.ds(p, 1)] = from_buf[g, pl.ds(p, 1)]

    def fill(to_buf, g, matrix, data):
        for part in range(4):
            rows = dot_nn(matrix[part * 256 : (part + 1) * 256, :], data)
            to_buf[g, part * 8 : (part + 1) * 8] = rows.astype(BF16).reshape(8, CAP, 2 * HD)

    for g in range(2):

        @pl.when(swapped)
        def _():
            swaps[2 * g].wait_recv()
            swaps[2 * g + 1].wait_recv()

        fill(sbuf, g, pack, xbuf[g])
        exchange(sbuf, rbuf, g, fwd_s, fwd_r)
    for copy in rims:
        copy.start()

    for g in range(2):
        wait_bytes(rbuf.at[g, pl.ds(0, NPLANE - 1)], fwd_r.at[g])
        xc[g] = dot_nn(sort[...], rbuf[g].reshape(SLOTS, 2 * HD)).astype(BF16)

    half = TOK // 2

    def cluster_rows(qb):
        lo = qb * half
        nk = lo + half
        query = xc[0, lo : lo + half, :HD]
        grad = xc[1, lo : lo + half, HD:]
        key = xc[0, :nk, HD:]
        value = xc[1, :nk, :HD]
        mask = iota((nk, half), 0) <= iota((nk, half), 1) + lo
        out, grad_query, weights, grad_scores, _ = attend_rows(query, grad, [(key, value, mask)])
        res[0, lo : lo + half, :HD] = out.astype(BF16)
        res[0, lo : lo + half, HD:] = grad_query.astype(BF16)
        return dot_nn(grad_scores[0], query), dot_nn(weights[0], grad)

    dk_a, dv_a = cluster_rows(0)
    dk_b, dv_b = cluster_rows(1)
    fill(sbuf2, 0, sort_t, res[0])
    exchange(sbuf2, rbuf2, 0, bwd_s, bwd_r)
    res[1, :half, :HD] = (dk_a + dk_b[:half]).astype(BF16)
    res[1, half:, :HD] = dk_b[half:].astype(BF16)
    res[1, :half, HD:] = (dv_a + dv_b[:half]).astype(BF16)
    res[1, half:, HD:] = dv_b[half:].astype(BF16)
    fill(sbuf2, 1, sort_t, res[1])
    exchange(sbuf2, rbuf2, 1, bwd_s, bwd_r)

    rims[0].wait_recv()
    rims[1].wait_recv()
    hide = jnp.where(seq == 0, 4 * TOK, 0)
    own_parts = []
    for qb in range(2):
        lo = qb * half
        nk = lo + half
        query = q_ref[lo : lo + half, :HD]
        grad = g_ref[lo : lo + half, :HD]
        behind = TOK - lo
        rim_mask = iota((behind, half), 0) + lo > iota((behind, half), 1) + lo + hide
        own_mask = iota((nk, half), 0) <= iota((nk, half), 1) + lo
        out, grad_query, weights, grad_scores, stats = attend_rows(
            query,
            grad,
            [
                (rim[0, lo:, :], rim[1, lo:, :], rim_mask),
                (k_ref[:nk, :HD], v_ref[:nk, :HD], own_mask),
            ],
        )
        o_ref[lo : lo + half, :HD] = out.astype(BF16)
        dq_ref[lo : lo + half, :HD] = grad_query.astype(BF16)
        for row, stat in enumerate(stats):
            stat_out[row : row + 1, lo : lo + half] = stat
        own_parts.append((dot_nn(grad_scores[1], query), dot_nn(weights[1], grad)))
    stats_copy = remote(stat_out, stat_in, stat_s, stat_r, prev_dev)
    stats_copy.start()

    targets = ((o_ref, dq_ref), (dk_ref, dv_ref))
    backs = [
        remote(bsend.at[g], brecv.at[g], back_s.at[g], back_r.at[g], swap_dev) for g in range(2)
    ]
    for g in range(2):
        wait_bytes(rbuf2.at[g, pl.ds(0, NPLANE - 1)], bwd_r.at[g])
        bsend[g] = dot_nn(pack_t[...], rbuf2[g].reshape(SLOTS, 2 * HD)).astype(BF16)

        @pl.when(swapped)
        def _():
            backs[g].start()

        @pl.when(jnp.logical_not(swapped))
        def _():
            targets[g][0][:, HD:] = bsend[g, :, :HD]
            targets[g][1][:, HD:] = bsend[g, :, HD:]

    rims[2].wait_recv()
    rims[3].wait_recv()
    stats_copy.wait_recv()
    last = jnp.where(seq == 31, 4 * TOK, 0)
    next_parts = []
    for qb in range(2):
        lo = qb * half
        behind = TOK - lo
        query = rim[2, lo : lo + half, :]
        grad = rim[3, lo : lo + half, :]
        key = k_ref[lo:, :HD]
        value = v_ref[lo:, :HD]
        mask = iota((behind, half), 0) > iota((behind, half), 1) + last
        score = jnp.where(mask, dot_nt(key, query) * SCALE, -jnp.inf)
        top, inverse, delta = [stat_in[row : row + 1, lo : lo + half] for row in range(3)]
        prob = jnp.exp(score - top) * inverse
        weight = prob.astype(BF16)
        grad_score = (prob * (dot_nt(value, grad) - delta) * SCALE).astype(BF16)
        next_parts.append((dot_nn(grad_score, query), dot_nn(weight, grad)))
    for t, ref in enumerate((dk_ref, dv_ref)):
        own_a, own_b = own_parts[0][t], own_parts[1][t]
        next_a, next_b = next_parts[0][t], next_parts[1][t]
        ref[:half, :HD] = (own_a + own_b[:half] + next_a[:half]).astype(BF16)
        ref[half:, :HD] = (own_b[half:] + next_a[half:] + next_b).astype(BF16)

    @pl.when(swapped)
    def _():
        for g in range(2):
            backs[g].wait_recv()
            targets[g][0][:, HD:] = brecv[g, :, :HD]
            targets[g][1][:, HD:] = brecv[g, :, HD:]
        for copy in swaps:
            copy.wait_send()
        for copy in backs:
            copy.wait_send()

    for copy in rims:
        copy.wait_send()
    stats_copy.wait_send()
    wait_bytes(colbuf.at[pl.ds(0, NCOL - 1)], col_s)
    wait_bytes(planebuf.at[pl.ds(0, NPLANE - 1)], plane_s)
    for g in range(2):
        wait_bytes(rbuf.at[g, pl.ds(0, NPLANE - 1)], fwd_s.at[g])
        wait_bytes(rbuf2.at[g, pl.ds(0, NPLANE - 1)], bwd_s.at[g])


def write_out(*refs):
    for src, dst in zip(refs[:4], refs[4:]):
        dst[...] = src[...]


def on_device(query_rows, key_rows, value_rows, out_grad, members):
    vmem = pl.BlockSpec(memory_space=pltpu.VMEM)
    shape = jax.ShapeDtypeStruct((TOK, 2 * HD), BF16)
    padded = pltpu.VMEM((2, NPLANE, CAP, 2 * HD), BF16)
    pair = pltpu.VMEM((2, TOK, 2 * HD), BF16)
    dma = pltpu.SemaphoreType.DMA
    results = pl.pallas_call(
        kernel,
        out_shape=(shape,) * 4,
        in_specs=[vmem] * 5,
        out_specs=(vmem,) * 4,
        scratch_shapes=[
            pltpu.VMEM((1, 1, 128), jnp.int32),
            pltpu.VMEM((NCOL, 1, 128), jnp.int32),
            pltpu.VMEM((8, 128), jnp.int32),
            pltpu.VMEM((NPLANE, 8, 128), jnp.int32),
            pltpu.VMEM((NPLANE, TOK), F32),
            pair,
            pltpu.VMEM((4, TOK, HD), BF16),
            pltpu.VMEM((8, TOK), F32),
            pltpu.VMEM((8, TOK), F32),
            pltpu.VMEM((SLOTS, TOK), BF16),
            pltpu.VMEM((TOK, SLOTS), BF16),
            pltpu.VMEM((TOK, SLOTS), BF16),
            pltpu.VMEM((SLOTS, TOK), BF16),
            padded, padded, pair, pair, padded, padded, pair, pair,
            dma, dma, dma, dma, dma((4,)), dma((4,)), dma((4,)), dma((4,)), dma, dma,
            dma((2,)), dma((2,)), dma((2,)), dma((2,)), dma((2,)), dma((2,)),
        ],
        compiler_params=pltpu.CompilerParams(collective_id=0, has_side_effects=True),
    )(query_rows, key_rows, value_rows, out_grad, members.reshape(1, 32))


    return pl.pallas_call(
        write_out,
        out_shape=(shape,) * 4,
        in_specs=[vmem] * 4,
        out_specs=(vmem,) * 4,
    )(*results)


def solution(mesh):
    fine = Mesh(mesh.devices.reshape(NX, NY, NZH, NZL, NCORE), AXES)
    rows, cols = ("x", "y", "zh"), ("zl", "core")
    spec = P(rows, cols)
    return jax.shard_map(
        on_device,
        mesh=fine,
        in_specs=(spec, spec, spec, spec, P(AXES)),
        out_specs=(spec,) * 4,
        check_vma=False,
    )
```

```python
import math

import jax
import jax.numpy as jnp
from jax import lax
from jax.experimental import pallas as pl
from jax.experimental.pallas import tpu as pltpu
from jax.sharding import Mesh
from jax.sharding import PartitionSpec as P

HD = 128
TOK = 512
CAP = 32
NX, NY, NZH, NZL, NCORE = 4, 4, 2, 8, 2
NPLANE = NX * NY * NCORE
NCOL = NZH * NZL
SLOTS = NPLANE * CAP
AXES = ("x", "y", "zh", "zl", "core")
MESH = pl.DeviceIdType.MESH
F32 = jnp.float32
BF16 = jnp.bfloat16
SCALE = 1.0 / math.sqrt(HD)


def iota(shape, dim):
    return lax.broadcasted_iota(jnp.int32, shape, dim)


def iotaf(shape, dim):
    return iota(shape, dim).astype(F32)


def dot_nn(a, b):
    return lax.dot_general(a, b, (((1,), (0,)), ((), ())), preferred_element_type=F32)


def dot_nt(a, b):
    return lax.dot_general(a, b, (((1,), (1,)), ((), ())), preferred_element_type=F32)


def dot_tn(a, b):
    return lax.dot_general(a, b, (((0,), (0,)), ((), ())), preferred_element_type=F32)


def attend_rows(query, grad, parts):
    scores = [jnp.where(mask, dot_nt(key, query) * SCALE, -jnp.inf) for key, _, mask in parts]
    top = None
    for score in scores:
        part_top = jnp.max(score, axis=0, keepdims=True)
        top = part_top if top is None else jnp.maximum(top, part_top)
    terms = [jnp.exp(score - top) for score in scores]
    total = sum(jnp.sum(term, axis=0, keepdims=True) for term in terms)
    inverse = 1.0 / total
    probs = [term * inverse for term in terms]
    weights = [prob.astype(BF16) for prob in probs]
    grad_probs = [dot_nt(value, grad) for _, value, _ in parts]
    delta = sum(
        jnp.sum(prob * grad_prob, axis=0, keepdims=True)
        for prob, grad_prob in zip(probs, grad_probs)
    )
    grad_scores = [
        (prob * (grad_prob - delta) * SCALE).astype(BF16)
        for prob, grad_prob in zip(probs, grad_probs)
    ]
    out = sum(dot_tn(value, weight) for (_, value, _), weight in zip(parts, weights))
    grad_query = sum(dot_tn(key, gs) for (key, _, _), gs in zip(parts, grad_scores))
    return out.T, grad_query.T, weights, grad_scores, (top, inverse, delta)


def kernel(
    q_hbm, k_hbm, v_hbm, g_hbm, mem_ref,
    o_ref, dq_ref, dk_ref, dv_ref,
    q_ref, k_ref, v_ref, g_ref, load_s,
    piece, colbuf, tile, planebuf, lists,
    xbuf, rim, stat_out, stat_in,
    pack, pack_t, sort, sort_t,
    sbuf, rbuf, xc, res, sbuf2, rbuf2, bsend, brecv,
    col_s, col_r, plane_s, plane_r, swap_s, swap_r, rim_s, rim_r, stat_s, stat_r,
    fwd_s, fwd_r, bwd_s, bwd_r, back_s, back_r,
):
    x, y, zh, zl, core = [lax.axis_index(a) for a in AXES]
    z = zh * NZL + zl
    i = x * NY + y
    p = core * (NX * NY) + i
    seq = i * 2 + zh

    def in_plane(index):
        spot = lax.rem(index, NX * NY)
        return (spot // NY, lax.rem(spot, NY), zh, zl, index // (NX * NY))

    def in_column(depth):
        return (x, y, depth // NZL, lax.rem(depth, NZL), core)

    def of_seq(index):
        spot = index // 2
        return (spot // NY, lax.rem(spot, NY), lax.rem(index, 2), zl, core)

    swap_dev = (x, y, 1 - zh, zl, 1 - core)
    next_dev = of_seq(lax.rem(seq + 1, 32))
    prev_dev = of_seq(lax.rem(seq + 31, 32))
    far_dev = of_seq(lax.rem(seq + 31 + 2 * zh, 32))
    swapped = zh != core

    def remote(src, dst, send, recv, device):
        return pltpu.make_async_remote_copy(
            src_ref=src, dst_ref=dst, send_sem=send, recv_sem=recv,
            device_id=device, device_id_type=MESH,
        )

    def wait_bytes(ref, sem):
        pltpu.make_async_copy(ref, ref, sem).wait()

    h = zl * 2 + core
    loads = [
        pltpu.make_async_copy(src, dst, load_s.at[t])
        for t, (src, dst) in enumerate(
            ((q_hbm, q_ref), (k_hbm, k_ref), (v_hbm, v_ref), (g_hbm, g_ref))
        )
    ]
    for load in loads:
        load.start()

    stat_out[...] = jnp.zeros_like(stat_out)
    piece[0] = jnp.zeros((1, 128), jnp.int32)
    for quarter in range(4):

        @pl.when(lax.rem(h, 4) == quarter)
        def _():
            piece[0, :, quarter * 32 : quarter * 32 + 32] = mem_ref[...]


    barrier = pltpu.get_barrier_semaphore()

    def greet(device):
        pl.semaphore_signal(barrier, inc=1, device_id=device, device_id_type=MESH)

    greet(swap_dev)
    greet(far_dev)

    @pl.loop(1, NCOL)
    def _(d):
        greet(in_column(lax.rem(z + d, NCOL)))

    @pl.loop(1, NPLANE)
    def _(d):
        greet(in_plane(lax.rem(p + d, NPLANE)))

    pl.semaphore_wait(barrier, NCOL - 1 + NPLANE - 1 + 2)

    @pl.loop(1, NCOL)
    def _(d):
        remote(
            piece.at[0], colbuf.at[z], col_s, col_r, in_column(lax.rem(z + d, NCOL))
        ).start()

    for load in loads:
        load.wait()

    inputs = (q_ref, k_ref, v_ref, g_ref)
    route = pl.ds(HD, HD)
    local = pl.ds(0, HD)
    swaps = [
        remote(
            inputs[t].at[:, route],
            xbuf.at[t // 2, :, pl.ds((t % 2) * HD, HD)],
            swap_s.at[t], swap_r.at[t], swap_dev,
        )
        for t in range(4)
    ]
    rims = [
        remote(ref.at[:, local], rim.at[t], rim_s.at[t], rim_r.at[t], device)
        for t, (ref, device) in enumerate(
            ((k_ref, next_dev), (v_ref, next_dev), (q_ref, prev_dev), (g_ref, prev_dev))
        )
    ]

    @pl.when(swapped)
    def _():
        for copy in swaps:
            copy.start()

    @pl.when(jnp.logical_not(swapped))
    def _():
        for t in range(4):
            xbuf[t // 2, :, (t % 2) * HD : (t % 2 + 1) * HD] = inputs[t][:, HD:]

    colbuf[pl.ds(z, 1)] = piece[...]
    wait_bytes(colbuf.at[pl.ds(0, NCOL - 1)], col_r)
    for row in range(8):
        first = (row // 4) * NZL + (row % 4) * 2
        tile[row : row + 1, :] = colbuf[first] + colbuf[first + 1]

    @pl.loop(1, NPLANE)
    def _(d):
        remote(
            tile, planebuf.at[p], plane_s, plane_r, in_plane(lax.rem(p + d, NPLANE))
        ).start()

    planebuf[pl.ds(p, 1)] = tile[...][None]
    wait_bytes(planebuf.at[pl.ds(0, NPLANE - 1)], plane_r)
    for row in range(8):
        rows = planebuf[0:16, row, :] + planebuf[16:32, row, :]
        half, group = row // 4, row % 4
        lists[half * 16 : half * 16 + 16, group * 128 : (group + 1) * 128] = rows.astype(F32)

    base = ((2 * i + core) * TOK).astype(F32)

    @pl.loop(0, 8)
    def _(group):
        token_row = jnp.zeros((1, 128), F32)
        for member in range(4):
            cluster = group * 4 + member
            row = lists[pl.ds(cluster, 1), :]
            start = jnp.sum(jnp.where(row < base, 1.0, 0.0), axis=1, keepdims=True)
            wanted = iotaf((CAP, TOK), 0) + start
            picked = jnp.where(iotaf((CAP, TOK), 1) == wanted, row + 1.0, 0.0)
            token = jnp.sum(picked, axis=1, keepdims=True) - (1.0 + base)
            onehot = jnp.where(iotaf((CAP, TOK), 1) == token, 1.0, 0.0)
            pack[pl.ds(pl.multiple_of(cluster * CAP, CAP), CAP), :] = onehot.astype(BF16)
            placed = iota((CAP, 128), 1) == iota((CAP, 128), 0) + CAP * member
            token_row += jnp.sum(jnp.where(placed, token, 0.0), axis=0, keepdims=True)
        onehot = jnp.where(iotaf((TOK, 128), 0) == token_row, 1.0, 0.0)
        pack_t[:, pl.ds(pl.multiple_of(group * 128, 128), 128)] = onehot.astype(BF16)

    own = lists[pl.ds(p, 1), :].astype(jnp.int32)
    block = own >> 9
    same = iota((NPLANE, TOK), 0) == block
    earlier = jnp.sum(
        jnp.where(block < iota((NPLANE, TOK), 0), 1.0, 0.0), axis=1, keepdims=True
    )
    run_start = jnp.sum(jnp.where(same, earlier, 0.0), axis=0, keepdims=True)
    source = ((block & 1) * 16 + (block >> 1)) * CAP
    slot_row = source.astype(F32) + iotaf((1, TOK), 1) - run_start
    for part in range(8):
        rows = iotaf((128, TOK), 0) + part * 128.0
        sort_t[part * 128 : (part + 1) * 128, :] = jnp.where(rows == slot_row, 1.0, 0.0).astype(BF16)
    for part in range(4):
        piece_row = slot_row[:, part * 128 : (part + 1) * 128]
        diagonal = iota((128, 128), 0) == iota((128, 128), 1)
        slot_col = jnp.sum(jnp.where(diagonal, piece_row, 0.0), axis=1, keepdims=True)
        onehot = jnp.where(iotaf((128, SLOTS), 1) == slot_col, 1.0, 0.0)
        sort[part * 128 : (part + 1) * 128, :] = onehot.astype(BF16)


    def exchange(from_buf, to_buf, g, send, recv):
        @pl.loop(1, NPLANE)
        def _(d):
            other = lax.rem(p + d, NPLANE)
            remote(
                from_buf.at[g, other], to_buf.at[g, p], send.at[g], recv.at[g], in_plane(other)
            ).start()

        to_buf[g, pl.ds(p, 1)] = from_buf[g, pl.ds(p, 1)]

    def fill(to_buf, g, matrix, data):
        for part in range(4):
            rows = dot_nn(matrix[part * 256 : (part + 1) * 256, :], data)
            to_buf[g, part * 8 : (part + 1) * 8] = rows.astype(BF16).reshape(8, CAP, 2 * HD)

    for g in range(2):

        @pl.when(swapped)
        def _():
            swaps[2 * g].wait_recv()
            swaps[2 * g + 1].wait_recv()

        fill(sbuf, g, pack, xbuf[g])
        exchange(sbuf, rbuf, g, fwd_s, fwd_r)
    for copy in rims:
        copy.start()

    for g in range(2):
        wait_bytes(rbuf.at[g, pl.ds(0, NPLANE - 1)], fwd_r.at[g])
        xc[g] = dot_nn(sort[...], rbuf[g].reshape(SLOTS, 2 * HD)).astype(BF16)

    half = TOK // 2

    def cluster_rows(qb):
        lo = qb * half
        nk = lo + half
        query = xc[0, lo : lo + half, :HD]
        grad = xc[1, lo : lo + half, HD:]
        key = xc[0, :nk, HD:]
        value = xc[1, :nk, :HD]
        mask = iota((nk, half), 0) <= iota((nk, half), 1) + lo
        out, grad_query, weights, grad_scores, _ = attend_rows(query, grad, [(key, value, mask)])
        res[0, lo : lo + half, :HD] = out.astype(BF16)
        res[0, lo : lo + half, HD:] = grad_query.astype(BF16)
        return dot_nn(grad_scores[0], query), dot_nn(weights[0], grad)

    dk_a, dv_a = cluster_rows(0)
    dk_b, dv_b = cluster_rows(1)
    fill(sbuf2, 0, sort_t, res[0])
    exchange(sbuf2, rbuf2, 0, bwd_s, bwd_r)
    res[1, :half, :HD] = (dk_a + dk_b[:half]).astype(BF16)
    res[1, half:, :HD] = dk_b[half:].astype(BF16)
    res[1, :half, HD:] = (dv_a + dv_b[:half]).astype(BF16)
    res[1, half:, HD:] = dv_b[half:].astype(BF16)
    fill(sbuf2, 1, sort_t, res[1])
    exchange(sbuf2, rbuf2, 1, bwd_s, bwd_r)

    rims[0].wait_recv()
    rims[1].wait_recv()
    hide = jnp.where(seq == 0, 4 * TOK, 0)
    own_parts = []
    for qb in range(2):
        lo = qb * half
        nk = lo + half
        query = q_ref[lo : lo + half, :HD]
        grad = g_ref[lo : lo + half, :HD]
        behind = TOK - lo
        rim_mask = iota((behind, half), 0) + lo > iota((behind, half), 1) + lo + hide
        own_mask = iota((nk, half), 0) <= iota((nk, half), 1) + lo
        out, grad_query, weights, grad_scores, stats = attend_rows(
            query,
            grad,
            [
                (rim[0, lo:, :], rim[1, lo:, :], rim_mask),
                (k_ref[:nk, :HD], v_ref[:nk, :HD], own_mask),
            ],
        )
        o_ref[lo : lo + half, :HD] = out.astype(BF16)
        dq_ref[lo : lo + half, :HD] = grad_query.astype(BF16)
        for row, stat in enumerate(stats):
            stat_out[row : row + 1, lo : lo + half] = stat
        own_parts.append((dot_nn(grad_scores[1], query), dot_nn(weights[1], grad)))
    stats_copy = remote(stat_out, stat_in, stat_s, stat_r, prev_dev)
    stats_copy.start()

    targets = ((o_ref, dq_ref), (dk_ref, dv_ref))
    backs = [
        remote(bsend.at[g], brecv.at[g], back_s.at[g], back_r.at[g], swap_dev) for g in range(2)
    ]
    for g in range(2):
        wait_bytes(rbuf2.at[g, pl.ds(0, NPLANE - 1)], bwd_r.at[g])
        bsend[g] = dot_nn(pack_t[...], rbuf2[g].reshape(SLOTS, 2 * HD)).astype(BF16)

        @pl.when(swapped)
        def _():
            backs[g].start()

        @pl.when(jnp.logical_not(swapped))
        def _():
            targets[g][0][:, HD:] = bsend[g, :, :HD]
            targets[g][1][:, HD:] = bsend[g, :, HD:]

    rims[2].wait_recv()
    rims[3].wait_recv()
    stats_copy.wait_recv()
    last = jnp.where(seq == 31, 4 * TOK, 0)
    next_parts = []
    for qb in range(2):
        lo = qb * half
        behind = TOK - lo
        query = rim[2, lo : lo + half, :]
        grad = rim[3, lo : lo + half, :]
        key = k_ref[lo:, :HD]
        value = v_ref[lo:, :HD]
        mask = iota((behind, half), 0) > iota((behind, half), 1) + last
        score = jnp.where(mask, dot_nt(key, query) * SCALE, -jnp.inf)
        top, inverse, delta = [stat_in[row : row + 1, lo : lo + half] for row in range(3)]
        prob = jnp.exp(score - top) * inverse
        weight = prob.astype(BF16)
        grad_score = (prob * (dot_nt(value, grad) - delta) * SCALE).astype(BF16)
        next_parts.append((dot_nn(grad_score, query), dot_nn(weight, grad)))
    for t, ref in enumerate((dk_ref, dv_ref)):
        own_a, own_b = own_parts[0][t], own_parts[1][t]
        next_a, next_b = next_parts[0][t], next_parts[1][t]
        ref[:half, :HD] = (own_a + own_b[:half] + next_a[:half]).astype(BF16)
        ref[half:, :HD] = (own_b[half:] + next_a[half:] + next_b).astype(BF16)

    @pl.when(swapped)
    def _():
        for g in range(2):
            backs[g].wait_recv()
            targets[g][0][:, HD:] = brecv[g, :, :HD]
            targets[g][1][:, HD:] = brecv[g, :, HD:]
        for copy in swaps:
            copy.wait_send()
        for copy in backs:
            copy.wait_send()

    for copy in rims:
        copy.wait_send()
    stats_copy.wait_send()
    wait_bytes(colbuf.at[pl.ds(0, NCOL - 1)], col_s)
    wait_bytes(planebuf.at[pl.ds(0, NPLANE - 1)], plane_s)
    for g in range(2):
        wait_bytes(rbuf.at[g, pl.ds(0, NPLANE - 1)], fwd_s.at[g])
        wait_bytes(rbuf2.at[g, pl.ds(0, NPLANE - 1)], bwd_s.at[g])


def write_out(*refs):
    for src, dst in zip(refs[:4], refs[4:]):
        dst[...] = src[...]


def on_device(query_rows, key_rows, value_rows, out_grad, members):
    vmem = pl.BlockSpec(memory_space=pltpu.VMEM)
    hbm = pl.BlockSpec(memory_space=pltpu.HBM)
    block = pltpu.VMEM((TOK, 2 * HD), BF16)
    shape = jax.ShapeDtypeStruct((TOK, 2 * HD), BF16)
    padded = pltpu.VMEM((2, NPLANE, CAP, 2 * HD), BF16)
    pair = pltpu.VMEM((2, TOK, 2 * HD), BF16)
    dma = pltpu.SemaphoreType.DMA
    results = pl.pallas_call(
        kernel,
        out_shape=(shape,) * 4,
        in_specs=[hbm] * 4 + [vmem],
        out_specs=(vmem,) * 4,
        scratch_shapes=[
            block, block, block, block, pltpu.SemaphoreType.DMA((4,)),
            pltpu.VMEM((1, 1, 128), jnp.int32),
            pltpu.VMEM((NCOL, 1, 128), jnp.int32),
            pltpu.VMEM((8, 128), jnp.int32),
            pltpu.VMEM((NPLANE, 8, 128), jnp.int32),
            pltpu.VMEM((NPLANE, TOK), F32),
            pair,
            pltpu.VMEM((4, TOK, HD), BF16),
            pltpu.VMEM((8, TOK), F32),
            pltpu.VMEM((8, TOK), F32),
            pltpu.VMEM((SLOTS, TOK), BF16),
            pltpu.VMEM((TOK, SLOTS), BF16),
            pltpu.VMEM((TOK, SLOTS), BF16),
            pltpu.VMEM((SLOTS, TOK), BF16),
            padded, padded, pair, pair, padded, padded, pair, pair,
            dma, dma, dma, dma, dma((4,)), dma((4,)), dma((4,)), dma((4,)), dma, dma,
            dma((2,)), dma((2,)), dma((2,)), dma((2,)), dma((2,)), dma((2,)),
        ],
        compiler_params=pltpu.CompilerParams(
            collective_id=0, has_side_effects=True, vmem_limit_bytes=24 * 2**20
        ),
    )(
        *[
            pltpu.with_memory_space_constraint(rows, pltpu.HBM)
            for rows in (query_rows, key_rows, value_rows, out_grad)
        ],
        pltpu.with_memory_space_constraint(members.reshape(1, 32), pltpu.HBM),
    )


    return pl.pallas_call(
        write_out,
        out_shape=(shape,) * 4,
        in_specs=[vmem] * 4,
        out_specs=(vmem,) * 4,
        compiler_params=pltpu.CompilerParams(vmem_limit_bytes=8 * 2**20),
    )(*results)


def solution(mesh):
    fine = Mesh(mesh.devices.reshape(NX, NY, NZH, NZL, NCORE), AXES)
    rows, cols = ("x", "y", "zh"), ("zl", "core")
    spec = P(rows, cols)
    return jax.shard_map(
        on_device,
        mesh=fine,
        in_specs=(spec, spec, spec, spec, P(AXES)),
        out_specs=(spec,) * 4,
        check_vma=False,
    )
```

```python
import math

import jax
import jax.numpy as jnp
from jax import lax
from jax.experimental import pallas as pl
from jax.experimental.pallas import tpu as pltpu
from jax.sharding import Mesh
from jax.sharding import PartitionSpec as P

HD = 128
TOK = 512
CAP = 32
NX, NY, NZH, NZL, NCORE = 4, 4, 2, 8, 2
NPLANE = NX * NY * NCORE
NCOL = NZH * NZL
SLOTS = NPLANE * CAP
AXES = ("x", "y", "zh", "zl", "core")
MESH = pl.DeviceIdType.MESH
F32 = jnp.float32
BF16 = jnp.bfloat16
SCALE = 1.0 / math.sqrt(HD)


def iota(shape, dim):
    return lax.broadcasted_iota(jnp.int32, shape, dim)


def iotaf(shape, dim):
    return iota(shape, dim).astype(F32)


def dot_nn(a, b):
    return lax.dot_general(a, b, (((1,), (0,)), ((), ())), preferred_element_type=F32)


def dot_nt(a, b):
    return lax.dot_general(a, b, (((1,), (1,)), ((), ())), preferred_element_type=F32)


def dot_tn(a, b):
    return lax.dot_general(a, b, (((0,), (0,)), ((), ())), preferred_element_type=F32)


def attend_rows(query, grad, parts):
    scores = [jnp.where(mask, dot_nt(key, query) * SCALE, -jnp.inf) for key, _, mask in parts]
    top = None
    for score in scores:
        part_top = jnp.max(score, axis=0, keepdims=True)
        top = part_top if top is None else jnp.maximum(top, part_top)
    terms = [jnp.exp(score - top) for score in scores]
    total = sum(jnp.sum(term, axis=0, keepdims=True) for term in terms)
    inverse = 1.0 / total
    probs = [term * inverse for term in terms]
    weights = [prob.astype(BF16) for prob in probs]
    grad_probs = [dot_nt(value, grad) for _, value, _ in parts]
    delta = sum(
        jnp.sum(prob * grad_prob, axis=0, keepdims=True)
        for prob, grad_prob in zip(probs, grad_probs)
    )
    grad_scores = [
        (prob * (grad_prob - delta) * SCALE).astype(BF16)
        for prob, grad_prob in zip(probs, grad_probs)
    ]
    out = sum(dot_tn(value, weight) for (_, value, _), weight in zip(parts, weights))
    grad_query = sum(dot_tn(key, gs) for (key, _, _), gs in zip(parts, grad_scores))
    return out.T, grad_query.T, weights, grad_scores, (top, inverse, delta)


def kernel(
    q_hbm, k_hbm, v_hbm, g_hbm, mem_ref,
    o_ref, dq_ref, dk_ref, dv_ref,
    q_ref, k_ref, v_ref, g_ref, load_s,
    piece, colbuf, tile, planebuf, lists,
    xbuf, rim, stat_out, stat_in,
    pack, pack_t, sort, sort_t,
    sbuf, rbuf, xc, res, sbuf2, rbuf2, bsend, brecv,
    col_s, col_r, plane_s, plane_r, swap_s, swap_r, rim_s, rim_r, stat_s, stat_r,
    fwd_s, fwd_r, bwd_s, bwd_r, back_s, back_r,
):
    x, y, zh, zl, core = [lax.axis_index(a) for a in AXES]
    z = zh * NZL + zl
    i = x * NY + y
    p = core * (NX * NY) + i
    seq = i * 2 + zh

    def in_plane(index):
        spot = lax.rem(index, NX * NY)
        return (spot // NY, lax.rem(spot, NY), zh, zl, index // (NX * NY))

    def in_column(depth):
        return (x, y, depth // NZL, lax.rem(depth, NZL), core)

    def of_seq(index):
        spot = index // 2
        return (spot // NY, lax.rem(spot, NY), lax.rem(index, 2), zl, core)

    swap_dev = (x, y, 1 - zh, zl, 1 - core)
    next_dev = of_seq(lax.rem(seq + 1, 32))
    prev_dev = of_seq(lax.rem(seq + 31, 32))
    far_dev = of_seq(lax.rem(seq + 31 + 2 * zh, 32))
    swapped = zh != core

    def remote(src, dst, send, recv, device):
        return pltpu.make_async_remote_copy(
            src_ref=src, dst_ref=dst, send_sem=send, recv_sem=recv,
            device_id=device, device_id_type=MESH,
        )

    def wait_bytes(ref, sem):
        pltpu.make_async_copy(ref, ref, sem).wait()

    h = zl * 2 + core
    loads = [
        pltpu.make_async_copy(src, dst, load_s.at[t])
        for t, (src, dst) in enumerate(
            ((q_hbm, q_ref), (k_hbm, k_ref), (v_hbm, v_ref), (g_hbm, g_ref))
        )
    ]
    for load in loads:
        load.start()

    stat_out[...] = jnp.zeros_like(stat_out)
    piece[0] = jnp.zeros((1, 128), jnp.int32)
    for quarter in range(4):

        @pl.when(lax.rem(h, 4) == quarter)
        def _():
            piece[0, :, quarter * 32 : quarter * 32 + 32] = mem_ref[...]


    barrier = pltpu.get_barrier_semaphore()

    def greet(device):
        pl.semaphore_signal(barrier, inc=1, device_id=device, device_id_type=MESH)

    greet(swap_dev)
    greet(far_dev)

    @pl.loop(1, NCOL)
    def _(d):
        greet(in_column(lax.rem(z + d, NCOL)))

    @pl.loop(1, NPLANE)
    def _(d):
        greet(in_plane(lax.rem(p + d, NPLANE)))

    pl.semaphore_wait(barrier, NCOL - 1 + NPLANE - 1 + 2)

    @pl.loop(1, NCOL)
    def _(d):
        remote(
            piece.at[0], colbuf.at[z], col_s, col_r, in_column(lax.rem(z + d, NCOL))
        ).start()

    for load in loads:
        load.wait()

    inputs = (q_ref, k_ref, v_ref, g_ref)
    route = pl.ds(HD, HD)
    local = pl.ds(0, HD)
    swaps = [
        remote(
            inputs[t].at[:, route],
            xbuf.at[t // 2, :, pl.ds((t % 2) * HD, HD)],
            swap_s.at[t], swap_r.at[t], swap_dev,
        )
        for t in range(4)
    ]
    rims = [
        remote(ref.at[:, local], rim.at[t], rim_s.at[t], rim_r.at[t], device)
        for t, (ref, device) in enumerate(
            ((k_ref, next_dev), (v_ref, next_dev), (q_ref, prev_dev), (g_ref, prev_dev))
        )
    ]

    @pl.when(swapped)
    def _():
        for copy in swaps:
            copy.start()

    @pl.when(jnp.logical_not(swapped))
    def _():
        for t in range(4):
            xbuf[t // 2, :, (t % 2) * HD : (t % 2 + 1) * HD] = inputs[t][:, HD:]

    colbuf[pl.ds(z, 1)] = piece[...]
    wait_bytes(colbuf.at[pl.ds(0, NCOL - 1)], col_r)
    for row in range(8):
        first = (row // 4) * NZL + (row % 4) * 2
        tile[row : row + 1, :] = colbuf[first] + colbuf[first + 1]

    @pl.loop(1, NPLANE)
    def _(d):
        remote(
            tile, planebuf.at[p], plane_s, plane_r, in_plane(lax.rem(p + d, NPLANE))
        ).start()

    planebuf[pl.ds(p, 1)] = tile[...][None]
    wait_bytes(planebuf.at[pl.ds(0, NPLANE - 1)], plane_r)
    for row in range(8):
        rows = planebuf[0:16, row, :] + planebuf[16:32, row, :]
        half, group = row // 4, row % 4
        lists[half * 16 : half * 16 + 16, group * 128 : (group + 1) * 128] = rows.astype(F32)

    base = ((2 * i + core) * TOK).astype(F32)

    @pl.loop(0, 8)
    def _(group):
        token_row = jnp.zeros((1, 128), F32)
        for member in range(4):
            cluster = group * 4 + member
            row = lists[pl.ds(cluster, 1), :]
            start = jnp.sum(jnp.where(row < base, 1.0, 0.0), axis=1, keepdims=True)
            wanted = iotaf((CAP, TOK), 0) + start
            picked = jnp.where(iotaf((CAP, TOK), 1) == wanted, row + 1.0, 0.0)
            token = jnp.sum(picked, axis=1, keepdims=True) - (1.0 + base)
            onehot = jnp.where(iotaf((CAP, TOK), 1) == token, 1.0, 0.0)
            pack[pl.ds(pl.multiple_of(cluster * CAP, CAP), CAP), :] = onehot.astype(BF16)
            placed = iota((CAP, 128), 1) == iota((CAP, 128), 0) + CAP * member
            token_row += jnp.sum(jnp.where(placed, token, 0.0), axis=0, keepdims=True)
        onehot = jnp.where(iotaf((TOK, 128), 0) == token_row, 1.0, 0.0)
        pack_t[:, pl.ds(pl.multiple_of(group * 128, 128), 128)] = onehot.astype(BF16)

    own = lists[pl.ds(p, 1), :].astype(jnp.int32)
    block = own >> 9
    same = iota((NPLANE, TOK), 0) == block
    earlier = jnp.sum(
        jnp.where(block < iota((NPLANE, TOK), 0), 1.0, 0.0), axis=1, keepdims=True
    )
    run_start = jnp.sum(jnp.where(same, earlier, 0.0), axis=0, keepdims=True)
    source = ((block & 1) * 16 + (block >> 1)) * CAP
    slot_row = source.astype(F32) + iotaf((1, TOK), 1) - run_start
    for part in range(8):
        rows = iotaf((128, TOK), 0) + part * 128.0
        sort_t[part * 128 : (part + 1) * 128, :] = jnp.where(rows == slot_row, 1.0, 0.0).astype(BF16)
    for part in range(4):
        piece_row = slot_row[:, part * 128 : (part + 1) * 128]
        diagonal = iota((128, 128), 0) == iota((128, 128), 1)
        slot_col = jnp.sum(jnp.where(diagonal, piece_row, 0.0), axis=1, keepdims=True)
        onehot = jnp.where(iotaf((128, SLOTS), 1) == slot_col, 1.0, 0.0)
        sort[part * 128 : (part + 1) * 128, :] = onehot.astype(BF16)


    def exchange(from_buf, to_buf, g, send, recv):
        @pl.loop(1, NPLANE)
        def _(d):
            other = lax.rem(p + d, NPLANE)
            remote(
                from_buf.at[g, other], to_buf.at[g, p], send.at[g], recv.at[g], in_plane(other)
            ).start()

        to_buf[g, pl.ds(p, 1)] = from_buf[g, pl.ds(p, 1)]

    def fill(to_buf, g, matrix, data):
        for part in range(4):
            rows = dot_nn(matrix[part * 256 : (part + 1) * 256, :], data)
            to_buf[g, part * 8 : (part + 1) * 8] = rows.astype(BF16).reshape(8, CAP, 2 * HD)

    for g in range(2):

        @pl.when(swapped)
        def _():
            swaps[2 * g].wait_recv()
            swaps[2 * g + 1].wait_recv()

        fill(sbuf, g, pack, xbuf[g])
        exchange(sbuf, rbuf, g, fwd_s, fwd_r)
    for copy in rims:
        copy.start()

    for g in range(2):
        wait_bytes(rbuf.at[g, pl.ds(0, NPLANE - 1)], fwd_r.at[g])
        xc[g] = dot_nn(sort[...], rbuf[g].reshape(SLOTS, 2 * HD)).astype(BF16)

    half = TOK // 2

    def cluster_rows(qb):
        lo = qb * half
        nk = lo + half
        query = xc[0, lo : lo + half, :HD]
        grad = xc[1, lo : lo + half, HD:]
        key = xc[0, :nk, HD:]
        value = xc[1, :nk, :HD]
        mask = iota((nk, half), 0) <= iota((nk, half), 1) + lo
        out, grad_query, weights, grad_scores, _ = attend_rows(query, grad, [(key, value, mask)])
        res[0, lo : lo + half, :HD] = out.astype(BF16)
        res[0, lo : lo + half, HD:] = grad_query.astype(BF16)
        return dot_nn(grad_scores[0], query), dot_nn(weights[0], grad)

    dk_a, dv_a = cluster_rows(0)
    dk_b, dv_b = cluster_rows(1)
    fill(sbuf2, 0, sort_t, res[0])
    exchange(sbuf2, rbuf2, 0, bwd_s, bwd_r)
    res[1, :half, :HD] = (dk_a + dk_b[:half]).astype(BF16)
    res[1, half:, :HD] = dk_b[half:].astype(BF16)
    res[1, :half, HD:] = (dv_a + dv_b[:half]).astype(BF16)
    res[1, half:, HD:] = dv_b[half:].astype(BF16)
    fill(sbuf2, 1, sort_t, res[1])
    exchange(sbuf2, rbuf2, 1, bwd_s, bwd_r)

    targets = ((o_ref, dq_ref), (dk_ref, dv_ref))
    backs = [
        remote(bsend.at[g], brecv.at[g], back_s.at[g], back_r.at[g], swap_dev) for g in range(2)
    ]

    def give_back(g):
        wait_bytes(rbuf2.at[g, pl.ds(0, NPLANE - 1)], bwd_r.at[g])
        bsend[g] = dot_nn(pack_t[...], rbuf2[g].reshape(SLOTS, 2 * HD)).astype(BF16)

        @pl.when(swapped)
        def _():
            backs[g].start()

        @pl.when(jnp.logical_not(swapped))
        def _():
            targets[g][0][:, HD:] = bsend[g, :, :HD]
            targets[g][1][:, HD:] = bsend[g, :, HD:]

    give_back(0)

    rims[0].wait_recv()
    rims[1].wait_recv()
    hide = jnp.where(seq == 0, 4 * TOK, 0)
    own_parts = []
    for qb in range(2):
        lo = qb * half
        nk = lo + half
        query = q_ref[lo : lo + half, :HD]
        grad = g_ref[lo : lo + half, :HD]
        behind = TOK - lo
        rim_mask = iota((behind, half), 0) + lo > iota((behind, half), 1) + lo + hide
        own_mask = iota((nk, half), 0) <= iota((nk, half), 1) + lo
        out, grad_query, weights, grad_scores, stats = attend_rows(
            query,
            grad,
            [
                (rim[0, lo:, :], rim[1, lo:, :], rim_mask),
                (k_ref[:nk, :HD], v_ref[:nk, :HD], own_mask),
            ],
        )
        o_ref[lo : lo + half, :HD] = out.astype(BF16)
        dq_ref[lo : lo + half, :HD] = grad_query.astype(BF16)
        for row, stat in enumerate(stats):
            stat_out[row : row + 1, lo : lo + half] = stat
        own_parts.append((dot_nn(grad_scores[1], query), dot_nn(weights[1], grad)))
    stats_copy = remote(stat_out, stat_in, stat_s, stat_r, prev_dev)
    stats_copy.start()

    give_back(1)

    rims[2].wait_recv()
    rims[3].wait_recv()
    stats_copy.wait_recv()
    last = jnp.where(seq == 31, 4 * TOK, 0)
    next_parts = []
    for qb in range(2):
        lo = qb * half
        behind = TOK - lo
        query = rim[2, lo : lo + half, :]
        grad = rim[3, lo : lo + half, :]
        key = k_ref[lo:, :HD]
        value = v_ref[lo:, :HD]
        mask = iota((behind, half), 0) > iota((behind, half), 1) + last
        score = jnp.where(mask, dot_nt(key, query) * SCALE, -jnp.inf)
        top, inverse, delta = [stat_in[row : row + 1, lo : lo + half] for row in range(3)]
        prob = jnp.exp(score - top) * inverse
        weight = prob.astype(BF16)
        grad_score = (prob * (dot_nt(value, grad) - delta) * SCALE).astype(BF16)
        next_parts.append((dot_nn(grad_score, query), dot_nn(weight, grad)))
    for t, ref in enumerate((dk_ref, dv_ref)):
        own_a, own_b = own_parts[0][t], own_parts[1][t]
        next_a, next_b = next_parts[0][t], next_parts[1][t]
        ref[:half, :HD] = (own_a + own_b[:half] + next_a[:half]).astype(BF16)
        ref[half:, :HD] = (own_b[half:] + next_a[half:] + next_b).astype(BF16)

    @pl.when(swapped)
    def _():
        for g in range(2):
            backs[g].wait_recv()
            targets[g][0][:, HD:] = brecv[g, :, :HD]
            targets[g][1][:, HD:] = brecv[g, :, HD:]
        for copy in swaps:
            copy.wait_send()
        for copy in backs:
            copy.wait_send()

    for copy in rims:
        copy.wait_send()
    stats_copy.wait_send()
    wait_bytes(colbuf.at[pl.ds(0, NCOL - 1)], col_s)
    wait_bytes(planebuf.at[pl.ds(0, NPLANE - 1)], plane_s)
    for g in range(2):
        wait_bytes(rbuf.at[g, pl.ds(0, NPLANE - 1)], fwd_s.at[g])
        wait_bytes(rbuf2.at[g, pl.ds(0, NPLANE - 1)], bwd_s.at[g])


def write_out(*refs):
    for src, dst in zip(refs[:4], refs[4:]):
        dst[...] = src[...]


def on_device(query_rows, key_rows, value_rows, out_grad, members):
    vmem = pl.BlockSpec(memory_space=pltpu.VMEM)
    hbm = pl.BlockSpec(memory_space=pltpu.HBM)
    block = pltpu.VMEM((TOK, 2 * HD), BF16)
    shape = jax.ShapeDtypeStruct((TOK, 2 * HD), BF16)
    padded = pltpu.VMEM((2, NPLANE, CAP, 2 * HD), BF16)
    pair = pltpu.VMEM((2, TOK, 2 * HD), BF16)
    dma = pltpu.SemaphoreType.DMA
    results = pl.pallas_call(
        kernel,
        out_shape=(shape,) * 4,
        in_specs=[hbm] * 4 + [vmem],
        out_specs=(vmem,) * 4,
        scratch_shapes=[
            block, block, block, block, pltpu.SemaphoreType.DMA((4,)),
            pltpu.VMEM((1, 1, 128), jnp.int32),
            pltpu.VMEM((NCOL, 1, 128), jnp.int32),
            pltpu.VMEM((8, 128), jnp.int32),
            pltpu.VMEM((NPLANE, 8, 128), jnp.int32),
            pltpu.VMEM((NPLANE, TOK), F32),
            pair,
            pltpu.VMEM((4, TOK, HD), BF16),
            pltpu.VMEM((8, TOK), F32),
            pltpu.VMEM((8, TOK), F32),
            pltpu.VMEM((SLOTS, TOK), BF16),
            pltpu.VMEM((TOK, SLOTS), BF16),
            pltpu.VMEM((TOK, SLOTS), BF16),
            pltpu.VMEM((SLOTS, TOK), BF16),
            padded, padded, pair, pair, padded, padded, pair, pair,
            dma, dma, dma, dma, dma((4,)), dma((4,)), dma((4,)), dma((4,)), dma, dma,
            dma((2,)), dma((2,)), dma((2,)), dma((2,)), dma((2,)), dma((2,)),
        ],
        compiler_params=pltpu.CompilerParams(
            collective_id=0, has_side_effects=True, vmem_limit_bytes=24 * 2**20
        ),
    )(
        *[
            pltpu.with_memory_space_constraint(rows, pltpu.HBM)
            for rows in (query_rows, key_rows, value_rows, out_grad)
        ],
        pltpu.with_memory_space_constraint(members.reshape(1, 32), pltpu.HBM),
    )


    return pl.pallas_call(
        write_out,
        out_shape=(shape,) * 4,
        in_specs=[vmem] * 4,
        out_specs=(vmem,) * 4,
        compiler_params=pltpu.CompilerParams(vmem_limit_bytes=8 * 2**20),
    )(*results)


def solution(mesh):
    fine = Mesh(mesh.devices.reshape(NX, NY, NZH, NZL, NCORE), AXES)
    rows, cols = ("x", "y", "zh"), ("zl", "core")
    spec = P(rows, cols)
    return jax.shard_map(
        on_device,
        mesh=fine,
        in_specs=(spec, spec, spec, spec, P(AXES)),
        out_specs=(spec,) * 4,
        check_vma=False,
    )
```
